32 devices in a mesh: row: 4 (over y, core), col: 8 (over z, x).
Axes of the slice: x: 2, y: 2, z: 4, core: 2. Of those that a mesh axis runs over, the one named last changes fastest.
Arguments:
- factor: float32 [24, 262144], P(None, ('row', 'col')), may hold values from -1.2 to 1.2
- prior: float32 [24, 262144], P(None, ('row', 'col')), may hold values from -1.2 to 1.2
- tile_src: int32 [32, 384], P(('row', 'col')), may hold values from 0 to 63
- tile_dst: int32 [32, 384], P(('row', 'col')), may hold values from 0 to 63
- tile_count: int32 [32], P(('row', 'col')), may hold values from 96 to 384, as said below
- tile_vals: bfloat16 [12288, 128, 128], P(('row', 'col'))
- sep_idx: int32 [32, 4, 256], P(('row', 'col')), may hold values from 0 to 8191, as said below
- sep_count: int32 [32, 4], P(('row', 'col')), may hold values from 64 to 256, as said below
- couple: bfloat16 [32, 4, 256, 256], P(('row', 'col')), may hold values from -0.1875 to 0.1875
- masks: int32 [4], replicated, may hold values from 1 to 31, as said below
Outputs:
- new_factor: float32 [24, 262144], P(None, ('row', 'col'))
- momentum: float32 [], replicated
- energy: float32 [], replicated
The draws below stay inside these ranges and needn't reach their ends.
Inputs may be any that keep to these rules, and one draw needn't show every extreme that they name: `tile_count`: some partition has all 384 slots live; slots at or beyond a partition's count are padding. `sep_idx`: distinct within one partition and round. `sep_count`: in every round some partition has all 256 slots live. masks[0] is 31, masks[1] is 16 and the last round's mask is 1.
All inputs are finite; a program needn't handle non-finite values.
Results may differ from the reference program's by a relative error of at most 0.0031.
Values may be sent and summed in bfloat16 or wider, within the bound.
A program may use at most 128 MiB of HBM per device.

```python
import jax
import jax.numpy as jnp
from jax import lax

R = 24
TILE = 128
ROUNDS = 4
ITERS = 2
NODE_DEV = 8192
TILES_DEV = 384
SEP = 256
PARTS_SIZE = 32
NB = 64
NODES = 262144


def draw_tile_vals(key, part):
    position = jnp.arange(PARTS_SIZE, dtype=jnp.float32) / max(PARTS_SIZE - 1, 1)
    spread = 0.6 * (1.0 + 2.0 * position) / jnp.sqrt(5.0 * TILE)
    scaling = jnp.repeat(spread, TILES_DEV)[:, None, None]
    base = jax.random.normal(key, (PARTS_SIZE * TILES_DEV, TILE, TILE), jnp.float32)
    return (base * scaling).astype(jnp.bfloat16)


def draw_sep_idx(key, part):
    subkeys = jax.random.split(jax.random.fold_in(key, 11), PARTS_SIZE * ROUNDS)

    def pick_nodes(subkey):
        return jax.random.permutation(subkey, NODE_DEV)[:SEP]
    chosen = jax.vmap(pick_nodes)(subkeys)
    return chosen.reshape(PARTS_SIZE, ROUNDS, SEP).astype(jnp.int32)


def draw_sep_count(key, part):
    first_key = jax.random.fold_in(key, 21)
    second_key = jax.random.fold_in(key, 22)
    base = jax.random.randint(first_key, (PARTS_SIZE, ROUNDS), SEP // 4, SEP + 1)
    fullest = jax.random.randint(second_key, (ROUNDS,), 0, PARTS_SIZE)
    hit = jnp.arange(PARTS_SIZE, dtype=jnp.int32)[:, None] == fullest[None, :]
    return jnp.where(hit, SEP, base).astype(jnp.int32)


def draw_tile_count(key, part):
    first_key = jax.random.fold_in(key, 31)
    second_key = jax.random.fold_in(key, 32)
    shifts = jax.random.randint(first_key, (PARTS_SIZE,), 0, 3)
    base = jnp.right_shift(jnp.full((PARTS_SIZE,), TILES_DEV, jnp.int32), shifts)
    fullest = jax.random.randint(second_key, (), 0, PARTS_SIZE)
    return jnp.where(jnp.arange(PARTS_SIZE, dtype=jnp.int32) == fullest, TILES_DEV, base).astype(jnp.int32)


def draw_masks(key, part):
    middle = jax.random.randint(jax.random.fold_in(key, 41), (ROUNDS,), 1, PARTS_SIZE)
    middle = middle.at[0].set(PARTS_SIZE - 1)
    middle = middle.at[1].set(PARTS_SIZE // 2)
    middle = middle.at[ROUNDS - 1].set(1)
    return middle.astype(jnp.int32)


def place_ends(drawn, stream_key, low, largest):
    longest = drawn.shape.index(max(drawn.shape))
    spots = []
    for shift in (0, 1):
        where = [jax.random.randint(jax.random.fold_in(stream_key, axis), (), 0, length) for axis, length in enumerate(drawn.shape)]
        where[longest] = (where[longest] + shift) % drawn.shape[longest]
        spots.append(tuple(where))
    return drawn.at[spots[0]].set(low).at[spots[1]].set(largest)


def steps_of(stream_key, dims, shards, smallest, top_value):
    def one(dim, shards_of):
        heights = jax.random.uniform(jax.random.fold_in(jax.random.fold_in(stream_key, 6), dim), (shards_of,), jnp.float32, smallest / len(shards), top_value / len(shards))
        return jnp.repeat(jnp.exp(heights), dims[dim] // shards_of).reshape((-1,) + (1,) * (len(dims) - dim - 1))

    loudness = one(*shards[0])
    for cut in shards[1:]:
        loudness = loudness * one(*cut)
    return loudness


def scatter_about(own_key, dims, width, bound, cuts=(), kind=jnp.bfloat16):
    values = width * jax.random.normal(own_key, dims, jnp.float32)
    if cuts:
        values = values * steps_of(own_key, dims, cuts, -0.22, 0.18)
    return jnp.clip(values, -bound, bound).astype(kind)


def setup_inputs(seed: int = 0) -> dict:
    arg_keys = jax.random.split(jax.random.key(seed), 11)
    factor = scatter_about(arg_keys[0], (R, NODES), 0.2, 1.2, ((1, 32),), jnp.float32)
    prior = scatter_about(arg_keys[1], (R, NODES), 0.2, 1.2, ((1, 32),), jnp.float32)
    tile_src = place_ends(jax.random.randint(arg_keys[2], (PARTS_SIZE, TILES_DEV), 0, NB), jax.random.fold_in(arg_keys[2], 1), 0, NB - 1).astype(jnp.int32)
    tile_dst = place_ends(jax.random.randint(arg_keys[3], (PARTS_SIZE, TILES_DEV), 0, NB), jax.random.fold_in(arg_keys[3], 1), 0, NB - 1).astype(jnp.int32)
    tile_count = draw_tile_count(jax.random.fold_in(arg_keys[10], 71), 0)
    tile_vals = draw_tile_vals(jax.random.fold_in(arg_keys[10], 71), 0)
    sep_idx = draw_sep_idx(jax.random.fold_in(arg_keys[10], 71), 0)
    sep_count = draw_sep_count(jax.random.fold_in(arg_keys[10], 71), 0)
    couple = scatter_about(arg_keys[8], (PARTS_SIZE, ROUNDS, SEP, SEP), (4 * SEP) ** -0.5, 0.1875, ((0, 32),))
    masks = draw_masks(jax.random.fold_in(arg_keys[10], 71), 0)
    return {"factor": factor, "prior": prior, "tile_src": tile_src, "tile_dst": tile_dst, "tile_count": tile_count, "tile_vals": tile_vals, "sep_idx": sep_idx, "sep_count": sep_count, "couple": couple, "masks": masks}


MOMENTUM_CAP = 0.9

def tile_apply(inputs):
    grouped, sources, targets, live_count, values = inputs
    picked = jnp.take(grouped, sources, axis=1).astype(jnp.float32)
    products = jnp.einsum('rtk,tkc->rtc', picked, values.astype(jnp.float32), precision=lax.Precision.HIGHEST)
    live_tiles = (jnp.arange(sources.shape[0]) < live_count).astype(jnp.float32)
    dst_table = (targets[None, :] == jnp.arange(grouped.shape[1], dtype=jnp.int32)[:, None]).astype(jnp.float32) * live_tiles[None, :]
    return jnp.einsum('bt,rtc->rbc', dst_table, products, precision=lax.Precision.HIGHEST)

def add_columns(target, columns, extra):
    return target.at[:, columns].add(extra)

def operate(packed, tile_src, tile_dst, tile_count, tile_vals, sep_idx, sep_count, couple, masks):
    grouped_all = packed.reshape(R, PARTS_SIZE, NB, TILE).transpose(1, 0, 2, 3)
    values_all = tile_vals.reshape(PARTS_SIZE, TILES_DEV, TILE, TILE)
    applied_dev = lax.map(tile_apply, (grouped_all, tile_src, tile_dst, tile_count, values_all))
    applied_dev = applied_dev.reshape(PARTS_SIZE, R, NODE_DEV)
    packed_dev = packed.reshape(R, PARTS_SIZE, NODE_DEV).transpose(1, 0, 2)
    for rnd in range(ROUNDS):
        columns = sep_idx[:, rnd, :]
        keep = jnp.arange(SEP, dtype=jnp.int32)[None, :] < sep_count[:, rnd][:, None]
        picked = jnp.take_along_axis(packed_dev, columns[:, None, :], axis=2)
        sent = jnp.where(keep[:, None, :], picked, jnp.zeros_like(picked))
        partner = jnp.arange(PARTS_SIZE, dtype=jnp.int32) ^ masks[rnd]
        received = sent[partner].astype(jnp.float32)
        extra = jnp.einsum('prs,pst->prt', received, couple[:, rnd].astype(jnp.float32), precision=lax.Precision.HIGHEST)
        extra = jnp.where(keep[:, None, :], extra, jnp.zeros_like(extra))
        applied_dev = jax.vmap(add_columns)(applied_dev, columns, extra)
    return applied_dev.transpose(1, 0, 2).reshape(R, NODES)

def reference(factor, prior, tile_src, tile_dst, tile_count, tile_vals, sep_idx, sep_count, couple, masks):
    current = factor
    previous = prior
    beta = jnp.float32(0.5 * MOMENTUM_CAP)
    energy = jnp.float32(0.0)
    for iterate in range(ITERS):
        blend = current + beta * (current - previous)
        packed = blend.astype(jnp.bfloat16)
        applied = operate(packed, tile_src, tile_dst, tile_count, tile_vals, sep_idx, sep_count, couple, masks)
        moved = blend + applied
        length = jnp.sqrt(lax.optimization_barrier(jnp.sum(moved * moved, axis=0, keepdims=True)))
        updated = moved / jnp.maximum(length, 1.0)
        change = jnp.sum(applied * (updated - current))
        energy = jnp.sum(applied * updated) / NODES
        beta = MOMENTUM_CAP * 0.5 * (1.0 + jnp.tanh(change / NODES))
        previous = current
        current = updated
    return (current, beta, energy)
```

```python
import functools

import jax
import jax.numpy as jnp
from jax import lax
from jax.experimental import pallas as pl
from jax.experimental.pallas import tpu as pltpu
from jax.sharding import PartitionSpec as P

TILE = 128
WIDE = 2 * TILE
MOMENTUM_CAP = 0.9
MESH = pl.DeviceIdType.MESH
LIMIT = 60 * 1024 * 1024
UNROLL = 16
SPLIT = 2
GROUP = 8
PIECES = 8


def flip(x, j):
    bit = 1
    while bit <= j:
        if j & bit:
            x = x + bit * (1 - 2 * ((x // bit) % 2))
        bit *= 2
    return x


def above(n):
    return 1 << (n - 1).bit_length()


def kernel(rows, cols, nodes_all, *refs):
    refs = list(refs)
    take = lambda n: [refs.pop(0) for _ in range(n)]
    fac_h, pri_h, src_h, dst_h, live_h, vals_h, idx_h, cnt_h, cpl_h, masks_h = take(10)
    out_h, beta_ref, energy_ref = take(3)
    fac, pri, src, dst, live, vals, idx, cnt, cpl, masks = take(10)
    code_v, loc_v, code, loc, lt = take(5)
    blend3, upd3, app3, both16, pack, run1, run2 = take(7)
    sbuf, direct, picked, stat = take(4)
    bcol, brow = take(3), take(3)
    in_sem, vals_sem, table_sem, out_sem = take(4)
    d_send, d_recv, c_send, c_recv, r_send, r_recv, st_send, st_recv = take(8)

    parts = rows * cols
    comps, nodes = fac.shape
    blocks = nodes // TILE
    supers = nodes // WIDE
    tiles = vals.shape[0]
    rounds, slots = idx.shape
    f32, bf16 = jnp.float32, jnp.bfloat16
    r = lax.axis_index("row")
    c = lax.axis_index("col")

    barrier = pltpu.get_barrier_semaphore()
    everyone = [(jr, jc) for jr in range(rows) for jc in range(cols) if jr or jc]
    for jr, jc in everyone:
        pl.semaphore_signal(barrier, inc=1, device_id=(flip(r, jr), flip(c, jc)), device_id_type=MESH)

    pairs = [(idx_h.at[0], idx), (fac_h, fac), (pri_h, pri), (cnt_h, cnt), (src_h, src), (dst_h, dst), (live_h, live),
             (masks_h, masks), (cpl_h.at[0], cpl)]
    loads = [pltpu.make_async_copy(a, b, in_sem.at[i]) for i, (a, b) in enumerate(pairs)]
    piece = tiles // PIECES
    spans = [pl.ds(i * piece, piece) for i in range(PIECES)]
    vals_loads = [pltpu.make_async_copy(vals_h.at[s], vals.at[s], vals_sem.at[i]) for i, s in enumerate(spans)]
    for copy in loads + vals_loads:
        copy.start()

    def lanes(b):
        return pl.ds(pl.multiple_of(b * TILE, TILE), TILE)

    slot_range = lax.broadcasted_iota(jnp.int32, (comps, slots), 1)
    loads[0].wait()
    lane_range = lax.broadcasted_iota(jnp.int32, (WIDE, slots), 0)
    for k in range(rounds):
        lt[k] = jnp.where(lane_range == (idx[k:k + 1, :] & (WIDE - 1)), 1.0, 0.0).astype(bf16)

    def home(k):
        return jnp.broadcast_to(idx[k:k + 1, :] // WIDE, (comps, slots))

    beta0 = 0.5 * MOMENTUM_CAP
    loads[1].wait()
    loads[2].wait()
    span4 = 2 * WIDE

    def doubled(x):
        return jnp.concatenate([x[:, :WIDE], x[:, WIDE:]], axis=0).astype(bf16)

    def begin(q, carry):
        at = pl.ds(pl.multiple_of(q * span4, span4), span4)
        f = fac[:, at]
        b = f + beta0 * (f - pri[:, at])
        pack[0, q] = doubled(b)
        pack[1, q] = doubled(f)
        for i in range(4):
            part = slice(i * TILE, (i + 1) * TILE)
            blend3[4 * q + i] = b[:, part]
            both16[4 * q + i] = jnp.concatenate([b[:, part], f[:, part]], axis=0).astype(bf16)
        return carry

    lax.fori_loop(0, supers // 2, begin, 0, unroll=2)
    loads[3].wait()

    def fixed(k):
        if k == 0:
            return parts - 1
        if k == 1:
            return parts // 2
        return 1 if k == rounds - 1 else None

    loose = [k for k in range(rounds) if fixed(k) is None]
    firm = [k for k in range(rounds) if fixed(k) is not None]

    def gather(kind, k):
        one = lt[k]
        where = home(k)
        total = jnp.zeros((comps, slots), f32)
        step = GROUP // 2
        for q in range(0, supers // 2, step):
            rows_in = pack[kind, q:q + step].reshape(step * 2 * comps, WIDE)
            got = jnp.dot(rows_in, one, preferred_element_type=f32)
            for i in range(GROUP):
                total = jnp.where(where == 2 * q + i, got[i * comps:(i + 1) * comps], total)
        sbuf[kind, k] = jnp.where(slot_range < cnt[0, k], total, 0.0).astype(bf16)

    started = []

    def go(copy):
        copy.start()
        started.append(copy)

    def direct_copy(kind, k):
        mask = fixed(k)
        return pltpu.make_async_remote_copy(
            src_ref=sbuf.at[kind, k], dst_ref=direct.at[kind, k], send_sem=d_send.at[kind, k], recv_sem=d_recv.at[kind, k],
            device_id=(flip(r, mask // cols), flip(c, mask % cols)), device_id_type=MESH)

    def col_copy(kind, n, j):
        return pltpu.make_async_remote_copy(
            src_ref=sbuf.at[kind, loose[n]], dst_ref=bcol[kind].at[n, j], send_sem=c_send.at[kind, n, j],
            recv_sem=c_recv.at[kind, n, j], device_id=(r, flip(c, j)), device_id_type=MESH)

    def row_copy(kind, n, j):
        return pltpu.make_async_remote_copy(
            src_ref=picked.at[kind, n], dst_ref=brow[kind].at[n, j], send_sem=r_send.at[kind, n, j],
            recv_sem=r_recv.at[kind, n, j], device_id=(flip(r, j), c), device_id_type=MESH)

    def send_loose(kind):
        for n in range(len(loose)):
            for j in range(cols - 1, 0, -1):
                go(col_copy(kind, n, j))
            bcol[kind][n, 0] = sbuf[kind, loose[n]]

    def relay(kind):
        for n, k in enumerate(loose):
            for j in range(1, cols):
                col_copy(kind, n, j).wait_recv()
            picked[kind, n] = bcol[kind][n, masks[k] % cols]
            for j in range(rows - 1, 0, -1):
                go(row_copy(kind, n, j))
            brow[kind][n, 0] = picked[kind, n]

    def take_loose(kind, n):
        for j in range(1, rows):
            row_copy(kind, n, j).wait_recv()
        return brow[kind][n, masks[loose[n]] // cols]

    def take_firm(kind, k):
        direct_copy(kind, k).wait_recv()
        return direct[kind, k]

    def send_firm(kind):
        for k in firm:
            go(direct_copy(kind, k))

    def stat_copy(stage, jr, jc):
        j = jr * cols + jc
        return pltpu.make_async_remote_copy(
            src_ref=stat.at[stage, 0], dst_ref=stat.at[stage, j], send_sem=st_send.at[stage, j], recv_sem=st_recv.at[stage, j],
            device_id=(flip(r, jr), flip(c, jc)), device_id_type=MESH)

    def stat_send(stage, change, total):
        half = lax.broadcasted_iota(jnp.int32, (1, TILE), 1) < TILE // 2
        fold = lambda x: x + pltpu.roll(x, TILE // 2, 1)
        change = fold(jnp.sum(change, axis=0, keepdims=True))
        total = fold(jnp.sum(total, axis=0, keepdims=True))
        stat[stage, 0] = jnp.where(half, change, total)
        for jr, jc in reversed(everyone):
            go(stat_copy(stage, jr, jc))

    def stat_take(stage):
        for jr, jc in everyone:
            stat_copy(stage, jr, jc).wait_recv()
        every = [stat[stage, j] for j in range(parts)]
        while len(every) > 1:
            every = [every[i] + every[i + 1] for i in range(0, len(every), 2)]
        half = lax.broadcasted_iota(jnp.int32, (1, TILE), 1) < TILE // 2
        sums = every[0] / nodes_all
        change = jnp.sum(jnp.where(half, sums, 0.0), axis=1, keepdims=True)
        energy = jnp.sum(jnp.where(half, 0.0, sums), axis=1, keepdims=True)
        return MOMENTUM_CAP * 0.5 * (1.0 + jnp.tanh(change)), energy

    for k in loose:
        gather(0, k)
    for copy in loads[4:7]:
        copy.wait()
    tile_row = lax.broadcasted_iota(jnp.int32, (1, tiles), 1)
    room = above(tiles)
    inner = above(blocks)
    key = jnp.where(tile_row < live[0], dst[...], blocks)
    rank_key = key * room + tile_row
    packed_code = (key * inner + src[...]) * room + tile_row

    def upright(x):
        return jnp.broadcast_to(x, (8, tiles)).T[:, :1]

    count = lambda mask: jnp.sum(jnp.where(mask, 1, 0), axis=0, keepdims=True)
    rank = count(upright(rank_key) < rank_key)
    code_col = upright(packed_code)
    code_v[...] = jnp.sum(jnp.where(upright(rank) == tile_row, code_col, 0), axis=0, keepdims=True)
    key_col = code_col // (inner * room)
    block_row = lax.broadcasted_iota(jnp.int32, loc_v.shape, 1)
    loc_v[...] = jnp.where(count(key_col == block_row) > 0, count(key_col <= block_row) - 1, tiles)
    tables = [pltpu.make_async_copy(code_v, code, table_sem.at[0]), pltpu.make_async_copy(loc_v, loc, table_sem.at[1])]
    for copy in tables:
        copy.start()
    loads[7].wait()
    pl.semaphore_wait(barrier, len(everyone))
    send_loose(0)
    for k in firm:
        gather(0, k)
    send_firm(0)
    for k in loose + firm:
        gather(1, k)
    run1[tiles] = jnp.zeros((2 * comps, TILE), f32)
    run2[tiles] = jnp.zeros((comps, TILE), f32)
    for copy in tables + vals_loads:
        copy.wait()

    def run_tiles(run, source, start, stop, carry):
        def some(i, carry):
            acc, last = carry
            base = i * UNROLL
            for j in range(0, UNROLL, 2):
                codes = [code[0, base + j + h] for h in range(2)]
                keys = [v // (inner * room) for v in codes]
                x = jnp.concatenate([source((v // room) % inner) for v in codes], axis=0).astype(bf16)
                side = jnp.concatenate([vals[v % room] for v in codes], axis=1)
                got = jnp.dot(x, side, preferred_element_type=f32)
                n = x.shape[0] // 2
                for h in range(2):
                    acc = jnp.where(keys[h] == last, acc, 0.0) + got[h * n:(h + 1) * n, h * TILE:(h + 1) * TILE]
                    run[base + j + h] = acc
                    last = keys[h]
            return acc, last

        return lax.fori_loop(start, stop, some, carry)

    steps = tiles // UNROLL
    middle = steps // SPLIT
    carry = (jnp.zeros((2 * comps, TILE), f32), jnp.int32(-1))
    carry = run_tiles(run1, lambda s: both16[s], 0, middle, carry)
    relay(0)
    send_loose(1)
    send_firm(1)
    run_tiles(run1, lambda s: both16[s], middle, steps, carry)
    loads[8].wait()

    def extra(k, received):
        e = jnp.dot(received, cpl[k], preferred_element_type=f32)
        return jnp.where(slot_range < cnt[0, k], e, 0.0)

    def scatter(first, found):
        total = None
        for k, e in found:
            where = home(k)
            left = jnp.concatenate([jnp.where(where == first + i, e, 0.0) for i in range(GROUP)], axis=0).astype(bf16)
            got = lax.dot_general(left, lt[k], (((1,), (1,)), ((), ())), preferred_element_type=f32)
            total = got if total is None else total + got
        return lambda i: total[(i // 2) * comps:(i // 2 + 1) * comps, (i % 2) * TILE:(i % 2 + 1) * TILE]

    group_blocks = 2 * GROUP

    def partial(found, product):
        for g in range(0, supers, GROUP):
            at = scatter(g, found)
            for i in range(group_blocks):
                b = 2 * g + i
                app3[b] = product(b) + at(i)

    def finish(found, blend, old, keep, after):
        zero = jnp.zeros((comps, TILE), f32)
        change, total = zero, zero
        for g in range(0, supers, GROUP):
            at = scatter(g, found)
            news = []
            for i in range(group_blocks):
                b = 2 * g + i
                applied = app3[b] + at(i)
                moved = blend(b) + applied
                scale = lax.rsqrt(jnp.maximum(jnp.sum(moved * moved, axis=0, keepdims=True), 1.0))
                updated = moved * scale
                keep(b, updated)
                news.append(updated)
                change = change + applied * (updated - old(b))
                total = total + applied * updated
            after(g, news)
        return change, total

    old0 = lambda b: fac[:, b * TILE:(b + 1) * TILE]
    partial([(k, extra(k, take_firm(0, k))) for k in firm], lambda b: run1[loc[0, b], :comps])
    found = [(k, extra(k, take_loose(0, n))) for n, k in enumerate(loose)]

    def keep_upd(b, updated):
        upd3[b] = updated

    def pack_upd(g, news):
        for i in range(0, len(news), 4):
            pack[2, g // 2 + i // 4] = doubled(jnp.concatenate(news[i:i + 4], axis=1))

    change, total = finish(found, lambda b: blend3[b], old0, keep_upd, pack_upd)
    stat_send(0, change, total)

    for k in loose:
        gather(2, k)
    send_loose(2)
    for k in firm:
        gather(2, k)
    send_firm(2)
    carry = (jnp.zeros((comps, TILE), f32), jnp.int32(-1))
    run_tiles(run2, lambda s: upd3[s], 0, steps, carry)
    relay(1)
    relay(2)
    beta, _ = stat_take(0)

    def mix(new, old):
        return (1.0 + beta) * new - beta * old

    def mixed(get, k):
        return mix(get(2, k).astype(f32), get(1, k).astype(f32)).astype(bf16)

    partial([(k, extra(k, mixed(take_firm, k))) for k in firm],
            lambda b: mix(run2[loc[0, b]], run1[loc[0, b], comps:]))
    found = [(k, extra(k, mixed(take_loose, n))) for n, k in enumerate(loose)]
    outs = []

    def keep_out(b, updated):
        pri[:, b * TILE:(b + 1) * TILE] = updated

    def write_out(g, news):
        span = pl.ds(g * WIDE, GROUP * WIDE)
        copy = pltpu.make_async_copy(pri.at[:, span], out_h.at[:, span], out_sem.at[g // GROUP])
        copy.start()
        outs.append(copy)

    change, total = finish(found, lambda b: upd3[b] + beta * (upd3[b] - old0(b)), lambda b: upd3[b], keep_out, write_out)
    stat_send(1, change, total)
    beta, energy = stat_take(1)
    beta_ref[...] = jnp.broadcast_to(beta, beta_ref.shape)
    energy_ref[...] = jnp.broadcast_to(energy, energy_ref.shape)
    for copy in outs:
        copy.wait()
    for copy in started:
        copy.wait_send()


def local(rows, cols, factor, prior, tile_src, tile_dst, tile_count, tile_vals, sep_idx, sep_count, couple, masks):
    comps, nodes = factor.shape
    tiles = tile_src.shape[1]
    blocks = nodes // TILE
    supers = nodes // WIDE
    _, rounds, slots = sep_idx.shape
    parts = rows * cols
    loose = max(rounds - 3, 1)
    f32, bf16, i32 = jnp.float32, jnp.bfloat16, jnp.int32
    vm, sm, dma = pltpu.VMEM, pltpu.SMEM, pltpu.SemaphoreType.DMA
    table = -(-blocks // TILE) * TILE
    args = (factor, prior, tile_src, tile_dst, tile_count, tile_vals, sep_idx, sep_count, couple, masks)
    result, beta, energy = pl.pallas_call(
        functools.partial(kernel, rows, cols, nodes * parts),
        out_shape=[jax.ShapeDtypeStruct((comps, nodes), f32)] + [jax.ShapeDtypeStruct((1, TILE), f32)] * 2,
        in_specs=[pl.BlockSpec(memory_space=pl.ANY)] * len(args),
        out_specs=[pl.BlockSpec(memory_space=pl.ANY)] + [pl.BlockSpec(memory_space=pltpu.VMEM)] * 2,
        scratch_shapes=[
            vm((comps, nodes), f32), vm((comps, nodes), f32), vm((1, tiles), i32), vm((1, tiles), i32), sm((1,), i32),
            vm(tile_vals.shape, bf16), vm((rounds, slots), i32), sm((1, rounds), i32), vm((rounds, slots, slots), bf16), sm((rounds,), i32),
            vm((1, tiles), i32), vm((1, table), i32), sm((1, tiles), i32), sm((1, table), i32), vm((rounds, WIDE, slots), bf16),
            vm((blocks, comps, TILE), f32), vm((blocks, comps, TILE), f32), vm((blocks, comps, TILE), f32),
            vm((blocks, 2 * comps, TILE), bf16), vm((3, supers // 2, 2 * comps, WIDE), bf16),
            vm((tiles + 1, 2 * comps, TILE), f32), vm((tiles + 1, comps, TILE), f32),
            vm((3, rounds, comps, slots), bf16), vm((3, rounds, comps, slots), bf16),
            vm((3, loose, comps, slots), bf16), vm((2, parts, 1, TILE), f32),
            *[vm((loose, cols, comps, slots), bf16)] * 3, *[vm((loose, rows, comps, slots), bf16)] * 3,
            dma((9,)), dma((PIECES,)), dma((2,)), dma((supers // GROUP,)),
            dma((3, rounds)), dma((3, rounds)), dma((3, loose, cols)), dma((3, loose, cols)), dma((3, loose, rows)), dma((3, loose, rows)),
            dma((2, parts)), dma((2, parts)),
        ],
        compiler_params=pltpu.CompilerParams(collective_id=0, has_side_effects=True, vmem_limit_bytes=LIMIT),
        name="rounds",
    )(*args)
    return result, beta[0, 0], energy[0, 0]


def solution(mesh):
    rows, cols = mesh.shape["row"], mesh.shape["col"]
    whole = P(("row", "col"))
    in_specs = (
        P(None, ("row", "col")), P(None, ("row", "col")),
        P(("row", "col"), None), P(("row", "col"), None), whole,
        P(("row", "col"), None, None), P(("row", "col"), None, None), P(("row", "col"), None),
        P(("row", "col"), None, None, None), P(),
    )
    out_specs = (P(None, ("row", "col")), P(), P())
    return jax.shard_map(functools.partial(local, rows, cols), mesh=mesh, in_specs=in_specs, out_specs=out_specs, check_vma=False)
```

```python
import functools

import jax
import jax.numpy as jnp
from jax import lax
from jax.experimental import pallas as pl
from jax.experimental.pallas import tpu as pltpu
from jax.sharding import PartitionSpec as P

TILE = 128
WIDE = 2 * TILE
MOMENTUM_CAP = 0.9
MESH = pl.DeviceIdType.MESH
LIMIT = 48 * 1024 * 1024
UNROLL = 32
SPLIT = (3, 4)
GROUP = 8


def flip(x, j):
    bit = 1
    while bit <= j:
        if j & bit:
            x = x + bit * (1 - 2 * ((x // bit) % 2))
        bit *= 2
    return x


def above(n):
    return 1 << (n - 1).bit_length()


def kernel(rows, cols, nodes_all, *refs):
    refs = list(refs)
    take = lambda n: [refs.pop(0) for _ in range(n)]
    fac_h, pri_h, src_h, dst_h, live_h, vals_h, idx_h, cnt_h, cpl_h, masks_h = take(10)
    out_h, beta_ref, energy_ref = take(3)
    fac, pri, src, dst, live, vals, idx, cnt, cpl, masks = take(10)
    order_v, loc_v, order, loc, lt = take(5)
    blend3, upd3, app3, both16, pack, run1, run2 = take(7)
    sbuf, direct, picked, stat = take(4)
    bcol, brow = take(3), take(3)
    in_sem, table_sem, out_sem = take(3)
    d_send, d_recv, c_send, c_recv, r_send, r_recv, st_send, st_recv = take(8)

    parts = rows * cols
    comps, nodes = fac.shape
    blocks = nodes // TILE
    supers = nodes // WIDE
    tiles = vals.shape[0]
    rounds, slots = idx.shape
    f32, bf16 = jnp.float32, jnp.bfloat16
    r = lax.axis_index("row")
    c = lax.axis_index("col")

    barrier = pltpu.get_barrier_semaphore()
    everyone = [(jr, jc) for jr in range(rows) for jc in range(cols) if jr or jc]
    for jr, jc in everyone:
        pl.semaphore_signal(barrier, inc=1, device_id=(flip(r, jr), flip(c, jc)), device_id_type=MESH)

    pairs = [(idx_h.at[0], idx), (fac_h, fac), (pri_h, pri), (cnt_h, cnt), (src_h, src), (dst_h, dst), (live_h, live),
             (masks_h, masks), (cpl_h.at[0], cpl)]
    loads = [pltpu.make_async_copy(a, b, in_sem.at[i]) for i, (a, b) in enumerate(pairs)]
    loads.append(pltpu.make_async_copy(vals_h, vals, in_sem.at[len(pairs)]))
    for copy in loads:
        copy.start()

    def lanes(b):
        return pl.ds(pl.multiple_of(b * TILE, TILE), TILE)

    slot_range = lax.broadcasted_iota(jnp.int32, (comps, slots), 1)
    loads[0].wait()
    lane_range = lax.broadcasted_iota(jnp.int32, (WIDE, slots), 0)
    for k in range(rounds):
        lt[k] = jnp.where(lane_range == (idx[k:k + 1, :] & (WIDE - 1)), 1.0, 0.0).astype(bf16)

    def home(k):
        return jnp.broadcast_to(idx[k:k + 1, :] // WIDE, (comps, slots))

    beta0 = 0.5 * MOMENTUM_CAP
    loads[1].wait()
    loads[2].wait()
    span4 = 2 * WIDE

    def doubled(x):
        return jnp.concatenate([x[:, :WIDE], x[:, WIDE:]], axis=0).astype(bf16)

    def begin(q, carry):
        at = pl.ds(pl.multiple_of(q * span4, span4), span4)
        f = fac[:, at]
        b = f + beta0 * (f - pri[:, at])
        pack[0, q] = doubled(b)
        pack[1, q] = doubled(f)
        for i in range(4):
            part = slice(i * TILE, (i + 1) * TILE)
            blend3[4 * q + i] = b[:, part]
            both16[4 * q + i] = jnp.concatenate([b[:, part], f[:, part]], axis=0).astype(bf16)
        return carry

    lax.fori_loop(0, supers // 2, begin, 0, unroll=2)
    loads[3].wait()

    def fixed(k):
        if k == 0:
            return parts - 1
        if k == 1:
            return parts // 2
        return 1 if k == rounds - 1 else None

    loose = [k for k in range(rounds) if fixed(k) is None]
    firm = [k for k in range(rounds) if fixed(k) is not None]

    def gather(kind, k):
        one = lt[k]
        where = home(k)
        total = jnp.zeros((comps, slots), f32)
        step = GROUP // 2
        for q in range(0, supers // 2, step):
            rows_in = pack[kind, q:q + step].reshape(step * 2 * comps, WIDE)
            got = jnp.dot(rows_in, one, preferred_element_type=f32)
            for i in range(GROUP):
                total = jnp.where(where == 2 * q + i, got[i * comps:(i + 1) * comps], total)
        sbuf[kind, k] = jnp.where(slot_range < cnt[0, k], total, 0.0).astype(bf16)

    pending = []

    def remote(source, target, send_sem, recv_sem, place):
        return pltpu.make_async_remote_copy(
            src_ref=source, dst_ref=target, send_sem=send_sem, recv_sem=recv_sem, device_id=place, device_id_type=MESH)

    def whole(target, send_sem, recv_sem):
        return remote(target, target, send_sem, recv_sem, (flip(r, 1), c))

    def firm_whole(kind):
        return whole(direct.at[kind], d_send.at[kind], d_recv.at[kind])

    def send_firm(kind):
        for m, k in enumerate(firm):
            place = (flip(r, fixed(k) // cols), flip(c, fixed(k) % cols))
            remote(sbuf.at[kind, k], direct.at[kind, m], d_send.at[kind], d_recv.at[kind], place).start()
        pending.append(firm_whole(kind))

    def col_whole(kind, n):
        return whole(bcol[kind].at[n, pl.ds(1, cols - 1)], c_send.at[kind, n], c_recv.at[kind, n])

    def row_whole(kind, n):
        return whole(brow[kind].at[n, pl.ds(1, rows - 1)], r_send.at[kind, n], r_recv.at[kind, n])

    def send_loose(kind):
        for n, k in enumerate(loose):
            for j in range(cols - 1, 0, -1):
                remote(sbuf.at[kind, k], bcol[kind].at[n, j], c_send.at[kind, n], c_recv.at[kind, n], (r, flip(c, j))).start()
            pending.append(col_whole(kind, n))
            bcol[kind][n, 0] = sbuf[kind, k]

    def relay(kind):
        for n, k in enumerate(loose):
            col_whole(kind, n).wait_recv()
            picked[kind, n] = bcol[kind][n, masks[0, k] % cols]
            for j in range(rows - 1, 0, -1):
                remote(picked.at[kind, n], brow[kind].at[n, j], r_send.at[kind, n], r_recv.at[kind, n], (flip(r, j), c)).start()
            pending.append(row_whole(kind, n))
            brow[kind][n, 0] = picked[kind, n]

    def take_loose(kind):
        for n in range(len(loose)):
            row_whole(kind, n).wait_recv()
        return {k: brow[kind][n, masks[0, k] // cols] for n, k in enumerate(loose)}

    def take_firm(kind):
        firm_whole(kind).wait_recv()
        return {k: direct[kind, m] for m, k in enumerate(firm)}

    def stat_whole(stage):
        return whole(stat.at[stage, pl.ds(1, parts - 1)], st_send.at[stage], st_recv.at[stage])

    def stat_send(stage, change, total):
        half = lax.broadcasted_iota(jnp.int32, (1, TILE), 1) < TILE // 2
        fold = lambda x: x + pltpu.roll(x, TILE // 2, 1)
        change = fold(jnp.sum(change, axis=0, keepdims=True))
        total = fold(jnp.sum(total, axis=0, keepdims=True))
        stat[stage, 0] = jnp.where(half, change, total)
        for jr, jc in reversed(everyone):
            remote(stat.at[stage, 0], stat.at[stage, jr * cols + jc], st_send.at[stage], st_recv.at[stage], (flip(r, jr), flip(c, jc))).start()
        pending.append(stat_whole(stage))

    def stat_take(stage):
        stat_whole(stage).wait_recv()
        every = [stat[stage, j] for j in range(parts)]
        while len(every) > 1:
            every = [every[i] + every[i + 1] for i in range(0, len(every), 2)]
        half = lax.broadcasted_iota(jnp.int32, (1, TILE), 1) < TILE // 2
        sums = every[0] / nodes_all
        change = jnp.sum(jnp.where(half, sums, 0.0), axis=1, keepdims=True)
        energy = jnp.sum(jnp.where(half, 0.0, sums), axis=1, keepdims=True)
        return MOMENTUM_CAP * 0.5 * (1.0 + jnp.tanh(change)), energy

    for k in loose:
        gather(0, k)
    loads[7].wait()
    pl.semaphore_wait(barrier, len(everyone))
    send_loose(0)
    for k in firm:
        gather(0, k)
    send_firm(0)
    for copy in loads[4:7]:
        copy.wait()
    tile_row = lax.broadcasted_iota(jnp.int32, (1, tiles), 1)
    key = jnp.where(tile_row < live[0], dst[...], blocks)
    ones = lambda mask: jnp.where(mask, 1.0, 0.0)
    across = lambda a, b: lax.dot_general(a.astype(bf16), b.astype(bf16), (((1,), (1,)), ((), ())), preferred_element_type=f32)
    block_at = lax.broadcasted_iota(jnp.int32, (loc_v.shape[1], tiles), 0)
    same = ones(block_at == key)
    upto = ones(key <= block_at)
    left = lax.broadcasted_iota(jnp.int32, (tiles, tiles), 0)
    ahead = jnp.dot(same.astype(bf16), ones(left < tile_row).astype(bf16), preferred_element_type=f32)
    ends = jnp.sum(upto, axis=1, keepdims=True) - jnp.sum(same, axis=1, keepdims=True)
    rank = jnp.sum(same * (ahead + ends), axis=0, keepdims=True).astype(jnp.int32)
    columns = jnp.concatenate([tile_row // TILE, tile_row % TILE, src[...], key] + [tile_row] * 4, axis=0)
    sort = across(columns.astype(f32), ones(left == rank)).astype(jnp.int32)
    within = lambda x, n: jnp.minimum(jnp.maximum(x, 0), n)
    order_v[0:1, :] = within(sort[0:1] * TILE + sort[1:2], tiles - 1)
    order_v[1:2, :] = within(sort[2:3], blocks - 1)
    order_v[2:3, :] = jnp.where(sort[3:4] == pltpu.roll(sort, 1, 1)[3:4], 1, 0)
    unit = jnp.ones((8, tiles), f32)
    found_at = jnp.where(across(unit, same)[:1] > 0.0, across(unit, upto)[:1].astype(jnp.int32) - 1, tiles)
    loc_v[...] = within(found_at, tiles)
    tables = [pltpu.make_async_copy(order_v, order, table_sem.at[0]), pltpu.make_async_copy(loc_v, loc, table_sem.at[1])]
    for copy in tables:
        copy.start()
    for k in loose + firm:
        gather(1, k)
    run1[tiles] = jnp.zeros((2 * comps, TILE), f32)
    run2[tiles] = jnp.zeros((comps, TILE), f32)
    for copy in tables + loads[9:]:
        copy.wait()

    def run_tiles(run, source, start, stop, carry):
        def some(i, carry):
            base = i * UNROLL
            for j in range(0, UNROLL, 2):
                x = jnp.concatenate([source(order[1, base + j + h]) for h in range(2)], axis=0).astype(bf16)
                side = jnp.concatenate([vals[order[0, base + j + h]] for h in range(2)], axis=1)
                got = jnp.dot(x, side, preferred_element_type=f32)
                n = x.shape[0] // 2
                for h in range(2):
                    carry = jnp.where(order[2, base + j + h] > 0, carry, 0.0) + got[h * n:(h + 1) * n, h * TILE:(h + 1) * TILE]
                    run[base + j + h] = carry
            return carry

        return lax.fori_loop(start, stop, some, carry)

    steps = tiles // UNROLL
    middle = steps * SPLIT[0] // SPLIT[1]
    carry = jnp.zeros((2 * comps, TILE), f32)
    carry = run_tiles(run1, lambda s: both16[s], 0, middle, carry)
    relay(0)
    send_loose(1)
    send_firm(1)
    run_tiles(run1, lambda s: both16[s], middle, steps, carry)
    loads[8].wait()

    def extra(k, received):
        e = jnp.dot(received, cpl[k], preferred_element_type=f32)
        return jnp.where(slot_range < cnt[0, k], e, 0.0)

    def scatter(first, found):
        total = None
        for k, e in found:
            where = home(k)
            left = jnp.concatenate([jnp.where(where == first + i, e, 0.0) for i in range(GROUP)], axis=0).astype(bf16)
            got = lax.dot_general(left, lt[k], (((1,), (1,)), ((), ())), preferred_element_type=f32)
            total = got if total is None else total + got
        return lambda i: total[(i // 2) * comps:(i // 2 + 1) * comps, (i % 2) * TILE:(i % 2 + 1) * TILE]

    group_blocks = 2 * GROUP

    def partial(found, product):
        for g in range(0, supers, GROUP):
            at = scatter(g, found)
            for i in range(group_blocks):
                b = 2 * g + i
                app3[b] = product(b) + at(i)

    def finish(found, blend, old, keep, after):
        zero = jnp.zeros((comps, TILE), f32)
        change, total = zero, zero
        for g in range(0, supers, GROUP):
            at = scatter(g, found)
            news = []
            for i in range(group_blocks):
                b = 2 * g + i
                applied = app3[b] + at(i)
                moved = blend(b) + applied
                scale = lax.rsqrt(jnp.maximum(jnp.sum(moved * moved, axis=0, keepdims=True), 1.0))
                updated = moved * scale
                keep(b, updated)
                news.append(updated)
                change = change + applied * (updated - old(b))
                total = total + applied * updated
            after(g, news)
        return change, total

    old0 = lambda b: fac[:, b * TILE:(b + 1) * TILE]
    partial([(k, extra(k, got)) for k, got in take_firm(0).items()], lambda b: run1[loc[0, b], :comps])
    found = [(k, extra(k, got)) for k, got in take_loose(0).items()]

    def keep_upd(b, updated):
        upd3[b] = updated

    def pack_upd(g, news):
        for i in range(0, len(news), 4):
            pack[2, g // 2 + i // 4] = doubled(jnp.concatenate(news[i:i + 4], axis=1))

    change, total = finish(found, lambda b: blend3[b], old0, keep_upd, pack_upd)
    for k in loose:
        gather(2, k)
    send_loose(2)
    stat_send(0, change, total)
    for k in firm:
        gather(2, k)
    send_firm(2)
    relay(1)
    run_tiles(run2, lambda s: upd3[s], 0, steps, jnp.zeros((comps, TILE), f32))
    relay(2)
    beta, _ = stat_take(0)

    def mix(new, old):
        return (1.0 + beta) * new - beta * old

    def mixed(get):
        old = get(1)
        return {k: mix(new.astype(f32), old[k].astype(f32)).astype(bf16) for k, new in get(2).items()}

    partial([(k, extra(k, got)) for k, got in mixed(take_firm).items()],
            lambda b: mix(run2[loc[0, b]], run1[loc[0, b], comps:]))
    found = [(k, extra(k, got)) for k, got in mixed(take_loose).items()]
    outs = []

    def keep_out(b, updated):
        pri[:, b * TILE:(b + 1) * TILE] = updated

    def write_out(g, news):
        span = pl.ds(g * WIDE, GROUP * WIDE)
        copy = pltpu.make_async_copy(pri.at[:, span], out_h.at[:, span], out_sem.at[g // GROUP])
        copy.start()
        outs.append(copy)

    change, total = finish(found, lambda b: upd3[b] + beta * (upd3[b] - old0(b)), lambda b: upd3[b], keep_out, write_out)
    stat_send(1, change, total)
    beta, energy = stat_take(1)
    beta_ref[...] = jnp.broadcast_to(beta, beta_ref.shape)
    energy_ref[...] = jnp.broadcast_to(energy, energy_ref.shape)
    for copy in outs:
        copy.wait()
    for copy in pending:
        copy.wait_send()


def local(rows, cols, factor, prior, tile_src, tile_dst, tile_count, tile_vals, sep_idx, sep_count, couple, masks):
    comps, nodes = factor.shape
    tiles = tile_src.shape[1]
    blocks = nodes // TILE
    supers = nodes // WIDE
    _, rounds, slots = sep_idx.shape
    parts = rows * cols
    loose = max(rounds - 3, 1)
    f32, bf16, i32 = jnp.float32, jnp.bfloat16, jnp.int32
    vm, sm, dma = pltpu.VMEM, pltpu.SMEM, pltpu.SemaphoreType.DMA
    table = -(-blocks // TILE) * TILE
    args = (factor, prior, tile_src, tile_dst, tile_count, tile_vals, sep_idx, sep_count, couple, masks)
    args = [a if a.size == 1 else pltpu.with_memory_space_constraint(a[None] if a.ndim == 1 else a, pltpu.HBM) for a in args]
    result, beta, energy = pl.pallas_call(
        functools.partial(kernel, rows, cols, nodes * parts),
        out_shape=[jax.ShapeDtypeStruct((comps, nodes), f32)] + [jax.ShapeDtypeStruct((1, TILE), f32)] * 2,
        in_specs=[pl.BlockSpec(memory_space=pltpu.HBM)] * len(args),
        out_specs=[pl.BlockSpec(memory_space=pl.ANY)] + [pl.BlockSpec(memory_space=pltpu.VMEM)] * 2,
        scratch_shapes=[
            vm((comps, nodes), f32), vm((comps, nodes), f32), vm((1, tiles), i32), vm((1, tiles), i32), sm((1,), i32),
            vm(tile_vals.shape, bf16), vm((rounds, slots), i32), sm((1, rounds), i32), vm((rounds, slots, slots), bf16), sm((1, rounds), i32),
            vm((3, tiles), i32), vm((1, table), i32), sm((3, tiles), i32), sm((1, table), i32), vm((rounds, WIDE, slots), bf16),
            vm((blocks, comps, TILE), f32), vm((blocks, comps, TILE), f32), vm((blocks, comps, TILE), f32),
            vm((blocks, 2 * comps, TILE), bf16), vm((3, supers // 2, 2 * comps, WIDE), bf16),
            vm((tiles + 1, 2 * comps, TILE), f32), vm((tiles + 1, comps, TILE), f32),
            vm((3, rounds, comps, slots), bf16), vm((3, rounds - loose, comps, slots), bf16),
            vm((3, loose, comps, slots), bf16), vm((2, parts, 1, TILE), f32),
            *[vm((loose, cols, comps, slots), bf16)] * 3, *[vm((loose, rows, comps, slots), bf16)] * 3,
            dma((len(args),)), dma((2,)), dma((supers // GROUP,)),
            dma((3,)), dma((3,)), dma((3, loose)), dma((3, loose)), dma((3, loose)), dma((3, loose)), dma((2,)), dma((2,)),
        ],
        compiler_params=pltpu.CompilerParams(collective_id=0, has_side_effects=True, vmem_limit_bytes=LIMIT),
        name="rounds",
    )(*args)
    return result, beta[0, 0], energy[0, 0]


def solution(mesh):
    rows, cols = mesh.shape["row"], mesh.shape["col"]
    whole = P(("row", "col"))
    in_specs = (
        P(None, ("row", "col")), P(None, ("row", "col")),
        P(("row", "col"), None), P(("row", "col"), None), whole,
        P(("row", "col"), None, None), P(("row", "col"), None, None), P(("row", "col"), None),
        P(("row", "col"), None, None, None), P(),
    )
    out_specs = (P(None, ("row", "col")), P(), P())
    return jax.shard_map(functools.partial(local, rows, cols), mesh=mesh, in_specs=in_specs, out_specs=out_specs, check_vma=False)
```

```python
import functools

import jax
import jax.numpy as jnp
from jax import lax
from jax.experimental import pallas as pl
from jax.experimental.pallas import tpu as pltpu
from jax.sharding import PartitionSpec as P

TILE = 128
WIDE = 2 * TILE
MOMENTUM_CAP = 0.9
MESH = pl.DeviceIdType.MESH
LIMIT = 48 * 1024 * 1024
UNROLL = 128
GROUP = 8


def flip(x, j):
    bit = 1
    while bit <= j:
        if j & bit:
            x = x + bit * (1 - 2 * ((x // bit) % 2))
        bit *= 2
    return x


def above(n):
    return 1 << (n - 1).bit_length()


def kernel(rows, cols, nodes_all, turn, *refs):
    refs = list(refs)
    take = lambda n: [refs.pop(0) for _ in range(n)]
    fac_h, pri_h, src_h, dst_h, live_h, vals_h, idx_h, cnt_h, cpl_h, masks_h = take(10)
    out_ref, beta_ref, energy_ref = take(3)
    fac, pri, src, dst, live, vals, idx, cnt, cpl, masks = take(10)
    order_v, tid, sid, keep, loc, lt = take(6)
    blend3, upd3, app3, both16, pack, run1, run2 = take(7)
    sbuf, direct, stat = take(3)
    around = take(3)
    in_sem, table_sem = take(2)
    d_send, d_recv, l_send, l_recv, st_send, st_recv, ready = take(7)

    parts = rows * cols
    comps, nodes = fac.shape
    blocks = nodes // TILE
    supers = nodes // WIDE
    tiles = vals.shape[0]
    rounds, slots = idx.shape
    f32, bf16 = jnp.float32, jnp.bfloat16
    r = lax.axis_index("row")
    c = lax.axis_index("col")

    barrier = pltpu.get_barrier_semaphore()
    everyone = [(jr, jc) for jr in range(rows) for jc in range(cols) if jr or jc]
    direct_to = {(rows - 1, cols - 1), (rows // 2, 0), (0, 1)}
    ring = {(turn, j) for j in range(cols)} - {(0, 0)}
    greeted = sorted(direct_to | ring | {(0, j) for j in range(1, cols)} | {(j, 0) for j in range(1, rows)}, reverse=True)
    for jr, jc in greeted:
        pl.semaphore_signal(barrier, inc=1, device_id=(flip(r, jr), flip(c, jc)), device_id_type=MESH)

    pairs = [(idx_h.at[0], idx), (fac_h, fac), (pri_h, pri), (cnt_h, cnt), (src_h, src), (dst_h, dst), (live_h, live),
             (masks_h, masks), (cpl_h.at[0], cpl)]
    loads = [pltpu.make_async_copy(a, b, in_sem.at[i]) for i, (a, b) in enumerate(pairs)]
    loads.append(pltpu.make_async_copy(vals_h, vals, in_sem.at[len(pairs)]))
    for copy in loads:
        copy.start()

    def lanes(b):
        return pl.ds(pl.multiple_of(b * TILE, TILE), TILE)

    slot_range = lax.broadcasted_iota(jnp.int32, (comps, slots), 1)
    loads[0].wait()
    lane_range = lax.broadcasted_iota(jnp.int32, (WIDE, slots), 0)
    for k in range(rounds):
        lt[k] = jnp.where(lane_range == (idx[k:k + 1, :] & (WIDE - 1)), 1.0, 0.0).astype(bf16)

    def home(k):
        return jnp.broadcast_to(idx[k:k + 1, :] // WIDE, (comps, slots))

    beta0 = 0.5 * MOMENTUM_CAP
    loads[1].wait()
    loads[2].wait()
    span4 = 2 * WIDE

    def doubled(x):
        return jnp.concatenate([x[:, :WIDE], x[:, WIDE:]], axis=0).astype(bf16)

    def begin(q, carry):
        at = pl.ds(pl.multiple_of(q * span4, span4), span4)
        f = fac[:, at]
        b = f + beta0 * (f - pri[:, at])
        pack[0, q] = doubled(b)
        pack[1, q] = doubled(f)
        for i in range(4):
            part = slice(i * TILE, (i + 1) * TILE)
            blend3[4 * q + i] = b[:, part]
        return carry

    lax.fori_loop(0, supers // 2, begin, 0, unroll=2)
    loads[3].wait()

    def fixed(k):
        if k == 0:
            return parts - 1
        if k == 1:
            return parts // 2
        return 1 if k == rounds - 1 else None

    loose = [k for k in range(rounds) if fixed(k) is None]
    firm = [k for k in range(rounds) if fixed(k) is not None]

    def gather(kind, k):
        one = lt[k]
        where = home(k)
        total = jnp.zeros((comps, slots), f32)
        step = GROUP // 2
        for q in range(0, supers // 2, step):
            rows_in = pack[kind, q:q + step].reshape(step * 2 * comps, WIDE)
            got = jnp.dot(rows_in, one, preferred_element_type=f32)
            for i in range(GROUP):
                total = jnp.where(where == 2 * q + i, got[i * comps:(i + 1) * comps], total)
        total = jnp.where(slot_range < cnt[0, k], total, 0.0)
        sbuf[kind, k] = jnp.concatenate([total[:, i:i + TILE] for i in range(0, slots, TILE)], axis=0).astype(bf16)

    pending = []

    def remote(source, target, send_sem, recv_sem, place):
        return pltpu.make_async_remote_copy(
            src_ref=source, dst_ref=target, send_sem=send_sem, recv_sem=recv_sem, device_id=place, device_id_type=MESH)

    def whole(target, send_sem, recv_sem):
        return remote(target, target, send_sem, recv_sem, (flip(r, 1), c))

    def firm_whole(kind):
        return whole(direct.at[kind], d_send.at[kind], d_recv.at[kind])

    def send_firm(kind):
        for m, k in enumerate(firm):
            place = (flip(r, fixed(k) // cols), flip(c, fixed(k) % cols))
            remote(sbuf.at[kind, k], direct.at[kind, m], d_send.at[kind], d_recv.at[kind], place).start()
        pending.append(firm_whole(kind))

    def loose_whole(kind, n):
        first = 0 if turn else 1
        return whole(around[kind].at[n, pl.ds(first, cols - first)], l_send.at[kind, n], l_recv.at[kind, n])

    def send_loose(kind):
        for n, k in enumerate(loose):
            for j in range(cols - 1, -1, -1):
                if turn or j:
                    place = (flip(r, turn), flip(c, j))
                    remote(sbuf.at[kind, k], around[kind].at[n, j], l_send.at[kind, n], l_recv.at[kind, n], place).start()
                else:
                    around[kind][n, 0] = sbuf[kind, k]
            pending.append(loose_whole(kind, n))

    def take_loose(kind):
        for n in range(len(loose)):
            loose_whole(kind, n).wait_recv()
        return {k: around[kind][n, masks[0, k] % cols] for n, k in enumerate(loose)}

    def take_firm(kind):
        firm_whole(kind).wait_recv()
        return {k: direct[kind, m] for m, k in enumerate(firm)}

    def stat_whole(stage):
        return whole(stat.at[stage, pl.ds(1, parts - 1)], st_send.at[stage], st_recv.at[stage])

    def stat_send(stage, change, total):
        half = lax.broadcasted_iota(jnp.int32, (1, TILE), 1) < TILE // 2
        fold = lambda x: x + pltpu.roll(x, TILE // 2, 1)
        change = fold(jnp.sum(change, axis=0, keepdims=True))
        total = fold(jnp.sum(total, axis=0, keepdims=True))
        stat[stage, 0] = jnp.where(half, change, total)
        for jr, jc in reversed(everyone):
            remote(stat.at[stage, 0], stat.at[stage, jr * cols + jc], st_send.at[stage], st_recv.at[stage], (flip(r, jr), flip(c, jc))).start()
        pending.append(stat_whole(stage))

    def stat_take(stage):
        stat_whole(stage).wait_recv()
        every = [stat[stage, j] for j in range(parts)]
        while len(every) > 1:
            every = [every[i] + every[i + 1] for i in range(0, len(every), 2)]
        half = lax.broadcasted_iota(jnp.int32, (1, TILE), 1) < TILE // 2
        sums = every[0] / nodes_all
        change = jnp.sum(jnp.where(half, sums, 0.0), axis=1, keepdims=True)
        energy = jnp.sum(jnp.where(half, 0.0, sums), axis=1, keepdims=True)
        return MOMENTUM_CAP * 0.5 * (1.0 + jnp.tanh(change)), energy

    for k in loose:
        gather(0, k)
    loads[7].wait()
    pl.semaphore_wait(barrier, len(greeted))
    for j in range(1, rows):
        pl.semaphore_signal(ready, inc=1, device_id=(flip(r, j), c), device_id_type=MESH)
    send_loose(0)
    for k in firm:
        gather(0, k)
    send_firm(0)
    for copy in loads[4:7]:
        copy.wait()
    tile_row = lax.broadcasted_iota(jnp.int32, (1, tiles), 1)
    key = jnp.where(tile_row < live[0], dst[...], blocks)
    ones = lambda mask: jnp.where(mask, 1.0, 0.0)
    across = lambda a, b: lax.dot_general(a.astype(bf16), b.astype(bf16), (((1,), (1,)), ((), ())), preferred_element_type=f32)
    block_at = lax.broadcasted_iota(jnp.int32, (max(TILE, blocks), tiles), 0)
    same = ones(block_at == key)
    upto = ones(key <= block_at)
    left = lax.broadcasted_iota(jnp.int32, (tiles, tiles), 0)
    ahead = jnp.dot(same.astype(bf16), ones(left < tile_row).astype(bf16), preferred_element_type=f32)
    ends = jnp.sum(upto, axis=1, keepdims=True) - jnp.sum(same, axis=1, keepdims=True)
    rank = jnp.sum(same * (ahead + ends), axis=0, keepdims=True).astype(jnp.int32)
    columns = jnp.concatenate([tile_row // TILE, tile_row % TILE, src[...], key] + [tile_row] * 4, axis=0)
    sort = across(columns.astype(f32), ones(left == rank)).astype(jnp.int32)
    within = lambda x, n: jnp.minimum(jnp.maximum(x, 0), n)
    order_v[0] = within(sort[0:1] * TILE + sort[1:2], tiles - 1)
    order_v[1] = within(sort[2:3], blocks - 1)
    order_v[2] = jnp.where(sort[3:4] == pltpu.roll(sort, 1, 1)[3:4], 1, 0)
    unit = jnp.ones((8, tiles), f32)
    found_at = jnp.where(across(unit, same)[:1] > 0.0, across(unit, upto)[:1].astype(jnp.int32) - 1, tiles)
    wide = jnp.concatenate([within(found_at, tiles)] * (-(-tiles // found_at.shape[1])), axis=1)
    order_v[3] = wide[:, :tiles]
    tables = [pltpu.make_async_copy(order_v.at[i, 0], t, table_sem.at[i]) for i, t in enumerate((tid, sid, keep, loc))]
    for copy in tables:
        copy.start()
    for k in loose + firm:
        gather(1, k)
    run1[tiles] = jnp.zeros((comps, TILE), f32)
    run2[tiles] = jnp.zeros((2 * comps, TILE), f32)
    for copy in tables + loads[9:]:
        copy.wait()

    def run_tiles(run, source, start, stop, carry):
        def some(i, carry):
            base = i * UNROLL
            for j in range(0, UNROLL, 2):
                x = jnp.concatenate([source(sid[base + j + h]) for h in range(2)], axis=0).astype(bf16)
                side = jnp.concatenate([vals[tid[base + j + h]] for h in range(2)], axis=1)
                got = jnp.dot(x, side, preferred_element_type=f32)
                n = x.shape[0] // 2
                for h in range(2):
                    carry = jnp.where(keep[base + j + h] > 0, carry, 0.0) + got[h * n:(h + 1) * n, h * TILE:(h + 1) * TILE]
                    run[base + j + h] = carry
            return carry

        return lax.fori_loop(start, stop, some, carry)

    send_loose(1)
    send_firm(1)
    steps = tiles // UNROLL
    run_tiles(run1, lambda s: blend3[s], 0, steps, jnp.zeros((comps, TILE), f32))
    loads[8].wait()

    def extra(k, received):
        e = 0.0
        for i in range(slots // TILE):
            e = e + jnp.dot(received, cpl[k, i * TILE:(i + 1) * TILE], preferred_element_type=f32)[i * comps:(i + 1) * comps]
        return jnp.where(slot_range < cnt[0, k], e, 0.0)

    def scatter(first, found):
        total = None
        for k, e in found:
            where = home(k)
            left = jnp.concatenate([jnp.where(where == first + i, e, 0.0) for i in range(GROUP)], axis=0).astype(bf16)
            got = lax.dot_general(left, lt[k], (((1,), (1,)), ((), ())), preferred_element_type=f32)
            total = got if total is None else total + got
        return lambda i: total[(i // 2) * comps:(i // 2 + 1) * comps, (i % 2) * TILE:(i % 2 + 1) * TILE]

    group_blocks = 2 * GROUP

    def partial(found, product):
        for g in range(0, supers, GROUP):
            at = scatter(g, found)
            for i in range(group_blocks):
                b = 2 * g + i
                app3[b] = product(b) + at(i)

    def finish(found, blend, old, keep, after):
        zero = jnp.zeros((comps, TILE), f32)
        change, total = zero, zero
        for g in range(0, supers, GROUP):
            at = scatter(g, found)
            news = []
            for i in range(group_blocks):
                b = 2 * g + i
                applied = app3[b] + at(i)
                moved = blend(b) + applied
                scale = lax.rsqrt(jnp.maximum(jnp.sum(moved * moved, axis=0, keepdims=True), 1.0))
                updated = moved * scale
                keep(b, updated)
                news.append(updated)
                change = change + applied * (updated - old(b))
                total = total + applied * updated
            after(g, news)
        return change, total

    old0 = lambda b: fac[:, b * TILE:(b + 1) * TILE]
    partial([(k, extra(k, got)) for k, got in take_firm(0).items()], lambda b: run1[loc[b]])
    found = [(k, extra(k, got)) for k, got in take_loose(0).items()]

    def keep_upd(b, updated):
        upd3[b] = updated
        both16[b] = jnp.concatenate([updated, old0(b)], axis=0).astype(bf16)

    def pack_upd(g, news):
        for i in range(0, len(news), 4):
            pack[2, g // 2 + i // 4] = doubled(jnp.concatenate(news[i:i + 4], axis=1))

    change, total = finish(found, lambda b: blend3[b], old0, keep_upd, pack_upd)
    pl.semaphore_wait(ready, rows - 1)
    stat_send(0, change, total)
    for k in loose:
        gather(2, k)
    send_loose(2)
    for k in firm:
        gather(2, k)
    send_firm(2)
    run_tiles(run2, lambda s: both16[s], 0, steps, jnp.zeros((2 * comps, TILE), f32))
    beta, _ = stat_take(0)

    def mix(new, old):
        return (1.0 + beta) * new - beta * old

    def mixed(get):
        old = get(1)
        return {k: mix(new.astype(f32), old[k].astype(f32)).astype(bf16) for k, new in get(2).items()}

    partial([(k, extra(k, got)) for k, got in mixed(take_firm).items()],
            lambda b: mix(run2[loc[b], :comps], run2[loc[b], comps:]))
    found = [(k, extra(k, got)) for k, got in mixed(take_loose).items()]

    def keep_out(b, updated):
        out_ref[:, b * TILE:(b + 1) * TILE] = updated

    change, total = finish(found, lambda b: upd3[b] + beta * (upd3[b] - old0(b)), lambda b: upd3[b], keep_out, lambda g, news: None)
    stat_send(1, change, total)
    beta, energy = stat_take(1)
    beta_ref[...] = jnp.broadcast_to(beta, beta_ref.shape)
    energy_ref[...] = jnp.broadcast_to(energy, energy_ref.shape)
    for copy in pending:
        copy.wait_send()


def local(rows, cols, factor, prior, tile_src, tile_dst, tile_count, tile_vals, sep_idx, sep_count, couple, masks):
    comps, nodes = factor.shape
    tiles = tile_src.shape[1]
    blocks = nodes // TILE
    supers = nodes // WIDE
    _, rounds, slots = sep_idx.shape
    parts = rows * cols
    loose = max(rounds - 3, 1)
    flat = (comps * slots // TILE, TILE)
    f32, bf16, i32 = jnp.float32, jnp.bfloat16, jnp.int32
    vm, sm, dma = pltpu.VMEM, pltpu.SMEM, pltpu.SemaphoreType.DMA
    args = (factor, prior, tile_src, tile_dst, tile_count, tile_vals, sep_idx, sep_count, couple, masks)
    args = [a if a.size == 1 else pltpu.with_memory_space_constraint(a[None] if a.ndim == 1 else a, pltpu.HBM) for a in args]
    run = lambda turn: pl.pallas_call(
        functools.partial(kernel, rows, cols, nodes * parts, turn),
        out_shape=[jax.ShapeDtypeStruct((comps, nodes), f32)] + [jax.ShapeDtypeStruct((1, TILE), f32)] * 2,
        in_specs=[pl.BlockSpec(memory_space=pltpu.HBM)] * len(args),
        out_specs=[pl.BlockSpec(memory_space=pltpu.VMEM)] * 3,
        scratch_shapes=[
            vm((comps, nodes), f32), vm((comps, nodes), f32), vm((1, tiles), i32), vm((1, tiles), i32), sm((1,), i32),
            vm(tile_vals.shape, bf16), vm((rounds, slots), i32), sm((1, rounds), i32), vm((rounds, slots, slots), bf16), sm((1, rounds), i32),
            vm((4, 1, tiles), i32), *[sm((tiles,), i32)] * 4, vm((rounds, WIDE, slots), bf16),
            vm((blocks, comps, TILE), f32), vm((blocks, comps, TILE), f32), vm((blocks, comps, TILE), f32),
            vm((blocks, 2 * comps, TILE), bf16), vm((3, supers // 2, 2 * comps, WIDE), bf16),
            vm((tiles + 1, comps, TILE), f32), vm((tiles + 1, 2 * comps, TILE), f32),
            vm((3, rounds, *flat), bf16), vm((3, rounds - loose, *flat), bf16),
            vm((2, parts, 1, TILE), f32),
            *[vm((loose, cols, *flat), bf16)] * 3,
            dma((len(args),)), dma((4,)),
            dma((3,)), dma((3,)), dma((3, loose)), dma((3, loose)), dma((2,)), dma((2,)), pltpu.SemaphoreType.REGULAR,
        ],
        compiler_params=pltpu.CompilerParams(collective_id=turn, has_side_effects=True, vmem_limit_bytes=LIMIT),
        name="rounds",
    )
    result, beta, energy = lax.switch(lax.shift_right_logical(masks[2], cols.bit_length() - 1), [run(turn) for turn in range(rows)], *args)
    return result, beta[0, 0], energy[0, 0]


def solution(mesh):
    rows, cols = mesh.shape["row"], mesh.shape["col"]
    whole = P(("row", "col"))
    in_specs = (
        P(None, ("row", "col")), P(None, ("row", "col")),
        P(("row", "col"), None), P(("row", "col"), None), whole,
        P(("row", "col"), None, None), P(("row", "col"), None, None), P(("row", "col"), None),
        P(("row", "col"), None, None, None), P(),
    )
    out_specs = (P(None, ("row", "col")), P(), P())
    return jax.shard_map(functools.partial(local, rows, cols), mesh=mesh, in_specs=in_specs, out_specs=out_specs, check_vma=False)
```

```python
import functools

import jax
import jax.numpy as jnp
from jax import lax
from jax.experimental import pallas as pl
from jax.experimental.pallas import tpu as pltpu
from jax.sharding import PartitionSpec as P

TILE = 128
WIDE = 2 * TILE
MOMENTUM_CAP = 0.9
MESH = pl.DeviceIdType.MESH
LIMIT = 48 * 1024 * 1024
UNROLL = 128
GROUP = 8


def flip(x, j):
    bit = 1
    while bit <= j:
        if j & bit:
            x = x + bit * (1 - 2 * ((x // bit) % 2))
        bit *= 2
    return x


def above(n):
    return 1 << (n - 1).bit_length()


def kernel(rows, cols, nodes_all, turn, *refs):
    refs = list(refs)
    take = lambda n: [refs.pop(0) for _ in range(n)]
    fac_h, pri_h, src_h, dst_h, live_h, vals_h, idx_h, cnt_h, cpl_h, masks_h = take(10)
    out_ref, beta_ref, energy_ref = take(3)
    fac, pri, src, dst, live, vals, idx, cnt, cpl, masks = take(10)
    order_v, tid, sid, keep, loc, lt = take(6)
    blend3, upd3, app3, both16, pack, run1, run2 = take(7)
    sbuf, direct, stat = take(3)
    around = take(3)
    in_sem, table_sem = take(2)
    d_send, d_recv, l_send, l_recv, st_send, st_recv, ready = take(7)

    parts = rows * cols
    comps, nodes = fac.shape
    blocks = nodes // TILE
    supers = nodes // WIDE
    tiles = vals.shape[0]
    rounds, slots = idx.shape
    f32, bf16 = jnp.float32, jnp.bfloat16
    r = lax.axis_index("row")
    c = lax.axis_index("col")

    barrier = pltpu.get_barrier_semaphore()
    everyone = [(jr, jc) for jr in range(rows) for jc in range(cols) if jr or jc]
    direct_to = {(rows - 1, cols - 1), (rows // 2, 0), (0, 1)}
    ring = {(turn, j) for j in range(cols)} - {(0, 0)}
    greeted = sorted(direct_to | ring | {(0, j) for j in range(1, cols)} | {(j, 0) for j in range(1, rows)}, reverse=True)
    for jr, jc in greeted:
        pl.semaphore_signal(barrier, inc=1, device_id=(flip(r, jr), flip(c, jc)), device_id_type=MESH)

    pairs = [(idx_h.at[0], idx), (fac_h, fac), (pri_h, pri), (cnt_h, cnt), (src_h, src), (dst_h, dst), (live_h, live),
             (masks_h, masks), (cpl_h.at[0], cpl)]
    loads = [pltpu.make_async_copy(a, b, in_sem.at[i]) for i, (a, b) in enumerate(pairs)]
    loads.append(pltpu.make_async_copy(vals_h, vals, in_sem.at[len(pairs)]))
    for copy in loads:
        copy.start()

    def lanes(b):
        return pl.ds(pl.multiple_of(b * TILE, TILE), TILE)

    slot_range = lax.broadcasted_iota(jnp.int32, (comps, slots), 1)
    loads[0].wait()
    lane_range = lax.broadcasted_iota(jnp.int32, (WIDE, slots), 0)
    for k in range(rounds):
        lt[k] = jnp.where(lane_range == (idx[k:k + 1, :] & (WIDE - 1)), 1.0, 0.0).astype(bf16)

    def home(k):
        return jnp.broadcast_to(idx[k:k + 1, :] // WIDE, (comps, slots))

    beta0 = 0.5 * MOMENTUM_CAP
    loads[1].wait()
    loads[2].wait()
    span4 = 2 * WIDE

    def doubled(x):
        return jnp.concatenate([x[:, :WIDE], x[:, WIDE:]], axis=0).astype(bf16)

    def begin(q, carry):
        at = pl.ds(pl.multiple_of(q * span4, span4), span4)
        f = fac[:, at]
        b = f + beta0 * (f - pri[:, at])
        pack[0, q] = doubled(b)
        pack[1, q] = doubled(f)
        for i in range(4):
            part = slice(i * TILE, (i + 1) * TILE)
            blend3[4 * q + i] = b[:, part]
        return carry

    lax.fori_loop(0, supers // 2, begin, 0, unroll=2)
    loads[3].wait()

    def fixed(k):
        if k == 0:
            return parts - 1
        if k == 1:
            return parts // 2
        return 1 if k == rounds - 1 else None

    loose = [k for k in range(rounds) if fixed(k) is None]
    firm = [k for k in range(rounds) if fixed(k) is not None]

    def gather(kind, k):
        one = lt[k]
        where = home(k)
        total = jnp.zeros((comps, slots), f32)
        step = GROUP // 2
        for q in range(0, supers // 2, step):
            rows_in = pack[kind, q:q + step].reshape(step * 2 * comps, WIDE)
            got = jnp.dot(rows_in, one, preferred_element_type=f32)
            for i in range(GROUP):
                total = jnp.where(where == 2 * q + i, got[i * comps:(i + 1) * comps], total)
        total = jnp.where(slot_range < cnt[0, k], total, 0.0)
        sbuf[kind, k] = jnp.concatenate([total[:, i:i + TILE] for i in range(0, slots, TILE)], axis=0).astype(bf16)

    pending = []

    def remote(source, target, send_sem, recv_sem, place):
        return pltpu.make_async_remote_copy(
            src_ref=source, dst_ref=target, send_sem=send_sem, recv_sem=recv_sem, device_id=place, device_id_type=MESH)

    def whole(target, send_sem, recv_sem):
        return remote(target, target, send_sem, recv_sem, (flip(r, 1), c))

    def firm_whole(kind):
        return whole(direct.at[kind], d_send.at[kind], d_recv.at[kind])

    def send_firm(kind, some):
        for k in some:
            place = (flip(r, fixed(k) // cols), flip(c, fixed(k) % cols))
            remote(sbuf.at[kind, k], direct.at[kind, firm.index(k)], d_send.at[kind], d_recv.at[kind], place).start()

    far, near = firm[:1], firm[1:]

    def loose_whole(kind, n):
        first = 0 if turn else 1
        return whole(around[kind].at[n, pl.ds(first, cols - first)], l_send.at[kind, n], l_recv.at[kind, n])

    def send_loose(kind):
        for n, k in enumerate(loose):
            for j in range(cols - 1, -1, -1):
                if turn or j:
                    place = (flip(r, turn), flip(c, j))
                    remote(sbuf.at[kind, k], around[kind].at[n, j], l_send.at[kind, n], l_recv.at[kind, n], place).start()
                else:
                    around[kind][n, 0] = sbuf[kind, k]
            pending.append(loose_whole(kind, n))

    def take_loose(kind):
        for n in range(len(loose)):
            loose_whole(kind, n).wait_recv()
        return {k: around[kind][n, masks[0, k] % cols] for n, k in enumerate(loose)}

    def take_firm(kind):
        firm_whole(kind).wait_recv()
        return {k: direct[kind, m] for m, k in enumerate(firm)}

    def stat_whole(stage):
        return whole(stat.at[stage, pl.ds(1, parts - 1)], st_send.at[stage], st_recv.at[stage])

    def stat_send(stage, change, total):
        half = lax.broadcasted_iota(jnp.int32, (1, TILE), 1) < TILE // 2
        fold = lambda x: x + pltpu.roll(x, TILE // 2, 1)
        change = fold(jnp.sum(change, axis=0, keepdims=True))
        total = fold(jnp.sum(total, axis=0, keepdims=True))
        stat[stage, 0] = jnp.where(half, change, total)
        for jr, jc in reversed(everyone):
            remote(stat.at[stage, 0], stat.at[stage, jr * cols + jc], st_send.at[stage], st_recv.at[stage], (flip(r, jr), flip(c, jc))).start()
        pending.append(stat_whole(stage))

    def stat_take(stage):
        stat_whole(stage).wait_recv()
        every = [stat[stage, j] for j in range(parts)]
        while len(every) > 1:
            every = [every[i] + every[i + 1] for i in range(0, len(every), 2)]
        half = lax.broadcasted_iota(jnp.int32, (1, TILE), 1) < TILE // 2
        sums = every[0] / nodes_all
        change = jnp.sum(jnp.where(half, sums, 0.0), axis=1, keepdims=True)
        energy = jnp.sum(jnp.where(half, 0.0, sums), axis=1, keepdims=True)
        return MOMENTUM_CAP * 0.5 * (1.0 + jnp.tanh(change)), energy

    for k in far + loose:
        gather(0, k)
    loads[7].wait()
    pl.semaphore_wait(barrier, len(greeted))
    for j in range(1, rows):
        pl.semaphore_signal(ready, inc=1, device_id=(flip(r, j), c), device_id_type=MESH)
    send_firm(0, far)
    send_loose(0)
    for k in near:
        gather(0, k)
    send_firm(0, near)
    pending.append(firm_whole(0))
    for copy in loads[4:7]:
        copy.wait()
    tile_row = lax.broadcasted_iota(jnp.int32, (1, tiles), 1)
    key = jnp.where(tile_row < live[0], dst[...], blocks)
    ones = lambda mask: jnp.where(mask, 1.0, 0.0)
    across = lambda a, b: lax.dot_general(a.astype(bf16), b.astype(bf16), (((1,), (1,)), ((), ())), preferred_element_type=f32)
    block_at = lax.broadcasted_iota(jnp.int32, (max(TILE, blocks), tiles), 0)
    same = ones(block_at == key)
    upto = ones(key <= block_at)
    left = lax.broadcasted_iota(jnp.int32, (tiles, tiles), 0)
    ahead = jnp.dot(same.astype(bf16), ones(left < tile_row).astype(bf16), preferred_element_type=f32)
    ends = jnp.sum(upto, axis=1, keepdims=True) - jnp.sum(same, axis=1, keepdims=True)
    rank = jnp.sum(same * (ahead + ends), axis=0, keepdims=True).astype(jnp.int32)
    columns = jnp.concatenate([tile_row // TILE, tile_row % TILE, src[...], key] + [tile_row] * 4, axis=0)
    sort = across(columns.astype(f32), ones(left == rank)).astype(jnp.int32)
    within = lambda x, n: jnp.minimum(jnp.maximum(x, 0), n)
    order_v[0] = within(sort[0:1] * TILE + sort[1:2], tiles - 1)
    order_v[1] = within(sort[2:3], blocks - 1)
    order_v[2] = jnp.where(sort[3:4] == pltpu.roll(sort, 1, 1)[3:4], 1, 0)
    unit = jnp.ones((8, tiles), f32)
    found_at = jnp.where(across(unit, same)[:1] > 0.0, across(unit, upto)[:1].astype(jnp.int32) - 1, tiles)
    wide = jnp.concatenate([within(found_at, tiles)] * (-(-tiles // found_at.shape[1])), axis=1)
    order_v[3] = wide[:, :tiles]
    tables = [pltpu.make_async_copy(order_v.at[i, 0], t, table_sem.at[i]) for i, t in enumerate((tid, sid, keep, loc))]
    for copy in tables:
        copy.start()
    for k in loose + firm:
        gather(1, k)
    run1[tiles] = jnp.zeros((comps, TILE), f32)
    run2[tiles] = jnp.zeros((2 * comps, TILE), f32)
    for copy in tables + loads[9:]:
        copy.wait()

    def run_tiles(run, source, start, stop, carry):
        def some(i, carry):
            base = i * UNROLL
            for j in range(0, UNROLL, 2):
                x = jnp.concatenate([source(sid[base + j + h]) for h in range(2)], axis=0).astype(bf16)
                side = jnp.concatenate([vals[tid[base + j + h]] for h in range(2)], axis=1)
                got = jnp.dot(x, side, preferred_element_type=f32)
                n = x.shape[0] // 2
                for h in range(2):
                    carry = jnp.where(keep[base + j + h] > 0, carry, 0.0) + got[h * n:(h + 1) * n, h * TILE:(h + 1) * TILE]
                    run[base + j + h] = carry
            return carry

        return lax.fori_loop(start, stop, some, carry)

    steps = tiles // UNROLL
    middle = steps * 2 // 3
    carry = run_tiles(run1, lambda s: blend3[s], 0, middle, jnp.zeros((comps, TILE), f32))
    send_loose(1)
    send_firm(1, firm)
    pending.append(firm_whole(1))
    run_tiles(run1, lambda s: blend3[s], middle, steps, carry)
    loads[8].wait()

    def extra(k, received):
        e = 0.0
        for i in range(slots // TILE):
            e = e + jnp.dot(received, cpl[k, i * TILE:(i + 1) * TILE], preferred_element_type=f32)[i * comps:(i + 1) * comps]
        return jnp.where(slot_range < cnt[0, k], e, 0.0)

    def scatter(first, found):
        total = None
        for k, e in found:
            where = home(k)
            left = jnp.concatenate([jnp.where(where == first + i, e, 0.0) for i in range(GROUP)], axis=0).astype(bf16)
            got = lax.dot_general(left, lt[k], (((1,), (1,)), ((), ())), preferred_element_type=f32)
            total = got if total is None else total + got
        return lambda i: total[(i // 2) * comps:(i // 2 + 1) * comps, (i % 2) * TILE:(i % 2 + 1) * TILE]

    group_blocks = 2 * GROUP

    def partial(found, product):
        for g in range(0, supers, GROUP):
            at = scatter(g, found)
            for i in range(group_blocks):
                b = 2 * g + i
                app3[b] = product(b) + at(i)

    def finish(found, blend, old, keep, after):
        zero = jnp.zeros((comps, TILE), f32)
        change, total = zero, zero
        for g in range(0, supers, GROUP):
            at = scatter(g, found)
            news = []
            for i in range(group_blocks):
                b = 2 * g + i
                applied = app3[b] + at(i)
                moved = blend(b) + applied
                scale = lax.rsqrt(jnp.maximum(jnp.sum(moved * moved, axis=0, keepdims=True), 1.0))
                updated = moved * scale
                keep(b, updated)
                news.append(updated)
                change = change + applied * (updated - old(b))
                total = total + applied * updated
            after(g, news)
        return change, total

    old0 = lambda b: fac[:, b * TILE:(b + 1) * TILE]
    partial([(k, extra(k, got)) for k, got in take_firm(0).items()], lambda b: run1[loc[b]])
    found = [(k, extra(k, got)) for k, got in take_loose(0).items()]

    def keep_upd(b, updated):
        upd3[b] = updated
        both16[b] = jnp.concatenate([updated, old0(b)], axis=0).astype(bf16)

    def pack_upd(g, news):
        for i in range(0, len(news), 4):
            pack[2, g // 2 + i // 4] = doubled(jnp.concatenate(news[i:i + 4], axis=1))

    change, total = finish(found, lambda b: blend3[b], old0, keep_upd, pack_upd)
    pl.semaphore_wait(ready, rows - 1)
    stat_send(0, change, total)
    for k in far:
        gather(2, k)
    send_firm(2, far)
    for k in loose:
        gather(2, k)
    send_loose(2)
    for k in near:
        gather(2, k)
    send_firm(2, near)
    pending.append(firm_whole(2))
    run_tiles(run2, lambda s: both16[s], 0, steps, jnp.zeros((2 * comps, TILE), f32))
    beta, _ = stat_take(0)

    def mix(new, old):
        return (1.0 + beta) * new - beta * old

    def mixed(get):
        old = get(1)
        return {k: mix(new.astype(f32), old[k].astype(f32)).astype(bf16) for k, new in get(2).items()}

    partial([(k, extra(k, got)) for k, got in mixed(take_firm).items()],
            lambda b: mix(run2[loc[b], :comps], run2[loc[b], comps:]))
    found = [(k, extra(k, got)) for k, got in mixed(take_loose).items()]

    def keep_out(b, updated):
        out_ref[:, b * TILE:(b + 1) * TILE] = updated

    change, total = finish(found, lambda b: upd3[b] + beta * (upd3[b] - old0(b)), lambda b: upd3[b], keep_out, lambda g, news: None)
    stat_send(1, change, total)
    beta, energy = stat_take(1)
    beta_ref[...] = jnp.broadcast_to(beta, beta_ref.shape)
    energy_ref[...] = jnp.broadcast_to(energy, energy_ref.shape)
    for copy in pending:
        copy.wait_send()


def local(rows, cols, factor, prior, tile_src, tile_dst, tile_count, tile_vals, sep_idx, sep_count, couple, masks):
    comps, nodes = factor.shape
    tiles = tile_src.shape[1]
    blocks = nodes // TILE
    supers = nodes // WIDE
    _, rounds, slots = sep_idx.shape
    parts = rows * cols
    loose = max(rounds - 3, 1)
    flat = (comps * slots // TILE, TILE)
    f32, bf16, i32 = jnp.float32, jnp.bfloat16, jnp.int32
    vm, sm, dma = pltpu.VMEM, pltpu.SMEM, pltpu.SemaphoreType.DMA
    args = (factor, prior, tile_src, tile_dst, tile_count, tile_vals, sep_idx, sep_count, couple, masks)
    args = [a if a.size == 1 else pltpu.with_memory_space_constraint(a[None] if a.ndim == 1 else a, pltpu.HBM) for a in args]
    run = lambda turn: pl.pallas_call(
        functools.partial(kernel, rows, cols, nodes * parts, turn),
        out_shape=[jax.ShapeDtypeStruct((comps, nodes), f32)] + [jax.ShapeDtypeStruct((1, TILE), f32)] * 2,
        in_specs=[pl.BlockSpec(memory_space=pltpu.HBM)] * len(args),
        out_specs=[pl.BlockSpec(memory_space=pltpu.VMEM)] * 3,
        scratch_shapes=[
            vm((comps, nodes), f32), vm((comps, nodes), f32), vm((1, tiles), i32), vm((1, tiles), i32), sm((1,), i32),
            vm(tile_vals.shape, bf16), vm((rounds, slots), i32), sm((1, rounds), i32), vm((rounds, slots, slots), bf16), sm((1, rounds), i32),
            vm((4, 1, tiles), i32), *[sm((tiles,), i32)] * 4, vm((rounds, WIDE, slots), bf16),
            vm((blocks, comps, TILE), f32), vm((blocks, comps, TILE), f32), vm((blocks, comps, TILE), f32),
            vm((blocks, 2 * comps, TILE), bf16), vm((3, supers // 2, 2 * comps, WIDE), bf16),
            vm((tiles + 1, comps, TILE), f32), vm((tiles + 1, 2 * comps, TILE), f32),
            vm((3, rounds, *flat), bf16), vm((3, rounds - loose, *flat), bf16),
            vm((2, parts, 1, TILE), f32),
            *[vm((loose, cols, *flat), bf16)] * 3,
            dma((len(args),)), dma((4,)),
            dma((3,)), dma((3,)), dma((3, loose)), dma((3, loose)), dma((2,)), dma((2,)), pltpu.SemaphoreType.REGULAR,
        ],
        compiler_params=pltpu.CompilerParams(collective_id=turn, has_side_effects=True, vmem_limit_bytes=LIMIT),
        name="rounds",
    )
    result, beta, energy = lax.switch(lax.shift_right_logical(masks[2], cols.bit_length() - 1), [run(turn) for turn in range(rows)], *args)
    return result, beta[0, 0], energy[0, 0]


def solution(mesh):
    rows, cols = mesh.shape["row"], mesh.shape["col"]
    whole = P(("row", "col"))
    in_specs = (
        P(None, ("row", "col")), P(None, ("row", "col")),
        P(("row", "col"), None), P(("row", "col"), None), whole,
        P(("row", "col"), None, None), P(("row", "col"), None, None), P(("row", "col"), None),
        P(("row", "col"), None, None, None), P(),
    )
    out_specs = (P(None, ("row", "col")), P(), P())
    return jax.shard_map(functools.partial(local, rows, cols), mesh=mesh, in_specs=in_specs, out_specs=out_specs, check_vma=False)
```
